32 devices in a mesh: rep: 2 (over x), seq: 16 (over z, y, core).
Axes of the slice: x: 2, y: 2, z: 4, core: 2. Of those that a mesh axis runs over, the one named last changes fastest.
Arguments:
- projected: bfloat16 [24576, 4096], P(('rep', 'seq')), parts along dimension 0, may hold values from -6 to 6
- history_in: bfloat16 [24576, 1024], P(('rep', 'seq')), parts along dimension 0, may hold values from -6 to 6
- norm_gain: float32 [1024], replicated, may hold values from 0.1 to 1.9
- out_proj: bfloat16 [1024, 1024], replicated, may hold values from -0.1875 to 0.1875
- user_spans: int32 [16], P('rep'), parts along dimension 0, may hold values from 1 to 4, as said below
- user_tails: int32 [16], P('rep'), parts along dimension 0, may hold values from 1 to 768
- cand_emb: bfloat16 [4096, 1024], P(('rep', 'seq')), parts along dimension 0, may hold values from -6 to 6
- cand_user: int32 [4096], P(('rep', 'seq')), parts along dimension 0, may hold values from 0 to 7
- cross_down: bfloat16 [2048, 128], replicated, may hold values from -0.125 to 0.125
- cross_up: bfloat16 [128, 2048], replicated, may hold values from -0.5 to 0.5
- cross_bias: float32 [2048], replicated, may hold values from -4 to 4
- score_weight: float32 [2048], replicated, may hold values from -0.125 to 0.125
Outputs:
- history_out: bfloat16 [24576, 1024], P(('rep', 'seq')), parts along dimension 0
- scores: float32 [4096], P(('rep', 'seq')), parts along dimension 0
The draws below stay inside these ranges and needn't reach their ends.
There are 2 independent parts, one for each index of `rep`. The reference program is written for one: setup_inputs(seed, part) draws one part's arguments, and reference() takes and returns one part's arrays. A program takes and returns all parts, laid end to end along the dimension named above; an argument that names none is the same for every part. Nothing has to cross between parts.
Inputs may be any that keep to these rules, and one draw needn't show every extreme that they name: `user_spans`: users own consecutive segments in order and together own all 16 segments; some user owns exactly 4.
All inputs are finite; a program needn't handle non-finite values.
Results may differ from the reference program's by a relative error of at most 0.0059.
Values may be sent and summed in bfloat16 or wider, within the bound.
A program may use at most 128 MiB of HBM per device.

```python
import jax
import jax.numpy as jnp
from jax import lax

D = 1024
HEADS = 8
RANK = 128
ROWS_DEV = 768
CAND_DEV = 128
SPAN = 4
USERS = 8
TOKENS = 12288
CANDS = 2048


def draw_user_spans(key, part):
    four_count = max(1, USERS // 8)
    three_count = USERS // 8
    one_count = 2 * four_count + three_count
    two_count = USERS - four_count - three_count - one_count
    pieces = [jnp.full((four_count,), 4, jnp.int32), jnp.full((one_count,), 1, jnp.int32)]
    if three_count > 0:
        pieces.append(jnp.full((three_count,), 3, jnp.int32))
    if two_count > 0:
        pieces.append(jnp.full((two_count,), 2, jnp.int32))
    spans = jnp.concatenate(pieces).astype(jnp.int32)
    return jax.random.permutation(jax.random.fold_in(key, 21), spans).astype(jnp.int32)


def touch_ends(result, stream_key, smallest, largest):
    spot = [jax.random.randint(jax.random.fold_in(stream_key, axis), (), 0, length) for axis, length in enumerate(result.shape)]
    longest = result.shape.index(max(result.shape))
    beside = spot[:longest] + [(spot[longest] + 1) % result.shape[longest]] + spot[longest + 1:]
    return result.at[tuple(spot)].set(smallest).at[tuple(beside)].set(largest)


def steps_of(key, shape, shards, low, top_value):
    loudness = 1.0
    for dim, blocks in shards:
        draws = jax.random.uniform(jax.random.fold_in(jax.random.fold_in(key, 6), dim), (blocks,), jnp.float32, low / len(shards), top_value / len(shards))
        loudness = loudness * jnp.repeat(jnp.exp(draws), shape[dim] // blocks).reshape((-1,) + (1,) * (len(shape) - 1 - dim))
    return loudness


def normal_values(stream_key, extent, width, reach, split=(), held_as=jnp.bfloat16):
    result = width * jax.random.normal(stream_key, extent, jnp.float32)
    if split:
        result = result * steps_of(stream_key, extent, split, -0.22, 0.18)
    return jnp.clip(result, -reach, reach).astype(held_as)


def setup_inputs(seed: int = 0, part: int = 0) -> dict:
    seeds = jax.random.split(jax.random.key(seed), 13)
    part_keys = jax.random.split(jax.random.fold_in(seeds[12], part), 13)
    return {
        "projected": normal_values(part_keys[0], (TOKENS, 4 * D), 1.0, 6.0, ((0, 16),)),
        "history_in": normal_values(part_keys[1], (TOKENS, D), 0.5, 6.0, ((0, 16),)),
        "norm_gain": jnp.clip(1.0 + 0.18 * jax.random.normal(seeds[2], (D,), jnp.float32), 0.1, 1.9),
        "out_proj": normal_values(seeds[3], (D, D), D ** -0.5, 0.1875),
        "user_spans": draw_user_spans(jax.random.fold_in(jax.random.fold_in(seeds[12], part), 71), part),
        "user_tails": touch_ends(jax.random.randint(part_keys[5], (USERS,), 1, ROWS_DEV + 1), jax.random.fold_in(part_keys[5], 1), 1, ROWS_DEV).astype(jnp.int32),
        "cand_emb": normal_values(part_keys[6], (CANDS, D), 1.0, 6.0, ((0, 16),)),
        "cand_user": touch_ends(jax.random.randint(part_keys[7], (CANDS,), 0, USERS), jax.random.fold_in(part_keys[7], 1), 0, USERS - 1).astype(jnp.int32),
        "cross_down": normal_values(seeds[8], (2 * D, RANK), (2 * D) ** -0.5, 0.125),
        "cross_up": normal_values(seeds[9], (RANK, 2 * D), RANK ** -0.5, 0.5),
        "cross_bias": normal_values(seeds[10], (2 * D,), 0.5, 4.0, (), jnp.float32),
        "score_weight": normal_values(seeds[11], (2 * D,), (2 * D) ** -0.5, 0.125, (), jnp.float32),
    }


def segment_owners(user_spans, user_tails, devices, row_count):
    last_dev = jnp.cumsum(user_spans).astype(jnp.int32) - 1
    first_dev = last_dev - user_spans.astype(jnp.int32) + 1
    device_ids = jnp.arange(devices, dtype=jnp.int32)
    owner_of = lax.optimization_barrier(jnp.sum((first_dev[None, :] <= device_ids[:, None]).astype(jnp.int32), axis=1)).astype(jnp.int32) - 1
    is_end = device_ids == last_dev[owner_of]
    valid_rows = jnp.where(is_end, user_tails[owner_of], row_count).astype(jnp.int32)
    return (last_dev, owner_of, valid_rows)

def reference(projected, history_in, norm_gain, out_proj, user_spans, user_tails, cand_emb, cand_user, cross_down, cross_up, cross_bias, score_weight):
    devices = USERS * 2
    row_count = ROWS_DEV
    model_width = D
    head_size = model_width // HEADS
    score_scale = head_size ** (-0.5)
    last_dev, owner_of, valid_rows = segment_owners(user_spans, user_tails, devices, row_count)
    blocks = projected.reshape(devices, row_count, 4 * model_width)
    residual_in = history_in.reshape(devices, row_count, model_width)
    row_ids = jnp.arange(row_count, dtype=jnp.int32)
    causal = (row_ids[None, :] <= row_ids[:, None]).astype(jnp.float32)

    def one_segment(my_index):
        own_block = blocks[my_index]
        queries = own_block[:, model_width:2 * model_width].reshape(row_count, HEADS, head_size).astype(jnp.float32)

        def attend(totals, source, weight_mask):
            key_values = blocks[source]
            key_part = key_values[:, 2 * model_width:3 * model_width].reshape(row_count, HEADS, head_size).astype(jnp.float32)
            value_part = key_values[:, 3 * model_width:].reshape(row_count, HEADS, head_size).astype(jnp.float32)
            logits = jnp.einsum('qhd,khd->hqk', queries, key_part) * score_scale
            weights = lax.optimization_barrier((jax.nn.silu(logits) * weight_mask).astype(jnp.bfloat16)).astype(jnp.float32)
            return totals + jnp.einsum('hqk,khd->qhd', weights, value_part)
        totals = attend(jnp.zeros((row_count, HEADS, head_size), jnp.float32), my_index, causal)

        def visit_block(offset, totals):
            source = (my_index - offset).astype(jnp.int32)
            clipped = jnp.maximum(source, 0).astype(jnp.int32)
            same_user = (source >= 0) & (owner_of[clipped] == owner_of[my_index])
            return lax.cond(same_user, lambda current: attend(current, clipped, jnp.float32(1.0)), lambda current: current, totals)
        totals = lax.fori_loop(1, SPAN, visit_block, totals)
        row_valid = (row_ids < valid_rows[my_index]).astype(jnp.float32)
        attention = totals.reshape(row_count, model_width) * row_valid[:, None]
        row_mean = lax.optimization_barrier(jnp.mean(attention, axis=1, keepdims=True))
        centered = attention - row_mean
        row_var = lax.optimization_barrier(jnp.mean(centered * centered, axis=1, keepdims=True))
        normed = centered * lax.rsqrt(row_var + 1e-06) * norm_gain
        gated = (normed * own_block[:, :model_width].astype(jnp.float32)).astype(jnp.bfloat16)
        return (jnp.dot(gated, out_proj, preferred_element_type=jnp.float32) + residual_in[my_index].astype(jnp.float32)).astype(jnp.bfloat16)
    history = lax.map(one_segment, jnp.arange(devices, dtype=jnp.int32))
    history_rows = history.reshape(devices * row_count, model_width)
    last_rows = (last_dev * row_count + user_tails - 1).astype(jnp.int32)
    user_rows = history_rows[last_rows]
    cand_blocks = cand_emb.reshape(devices, CAND_DEV, model_width)
    user_blocks = cand_user.reshape(devices, CAND_DEV)

    def score_block(pair):
        cand_rows, cand_users = pair
        crossed_in = jnp.concatenate([user_rows[cand_users], cand_rows], axis=1)
        low_rank = jnp.dot(crossed_in, cross_down, preferred_element_type=jnp.float32).astype(jnp.bfloat16)
        up_part = jnp.dot(low_rank, cross_up, preferred_element_type=jnp.float32)
        input_float = crossed_in.astype(jnp.float32)
        crossed = input_float * (up_part + cross_bias) + input_float
        return lax.optimization_barrier(jnp.sum(crossed * score_weight, axis=1))
    scores = lax.map(score_block, (cand_blocks, user_blocks)).reshape(devices * CAND_DEV)
    return (history_rows, scores)
```

```python
import functools

import jax
import jax.numpy as jnp
from jax import lax
from jax.experimental import pallas as pl
from jax.experimental.pallas import tpu as pltpu
from jax.sharding import PartitionSpec as P

HEADS = 8
MESH = pl.DeviceIdType.MESH
ONE_BACK, TWO_BACK, THREE_BACK, EVEN_OWN, OWN = range(5)


def history_kernel(
    n, row_tile, flags_ref, gain_ref, proj_ref, hist_ref, weight_ref, out_ref,
    kv, queries, gates, residual, weights, attn, local_sem, side_sem, send_sem, recv_sem,
):
    rep, me = lax.axis_index("rep"), lax.axis_index("seq")
    core = lax.rem(me, 2)
    side = lax.rem(me // 2, 2)
    rows, width = residual.shape
    size = width // HEADS
    half_scale = 0.5 * size ** (-0.5)

    def dev(shift):
        return lax.rem(me + shift + n, n)

    partner = me + 1 - 2 * core

    def load(h, part, target, sem):
        columns = pl.ds(pl.multiple_of(part * width + h * size, size), size)
        return pltpu.make_async_copy(proj_ref.at[:, columns], target, sem)

    def loads(h):
        return (
            load(h, 2, kv.at[OWN, h, 0], local_sem.at[h, 0]),
            load(h, 3, kv.at[OWN, h, 1], local_sem.at[h, 1]),
            load(h, 1, queries.at[h], local_sem.at[h, 2]),
        )

    late = (
        pltpu.make_async_copy(proj_ref.at[:, pl.ds(0, width)], gates, side_sem.at[0]),
        pltpu.make_async_copy(hist_ref, residual, side_sem.at[1]),
        pltpu.make_async_copy(weight_ref, weights, side_sem.at[2]),
    )

    @pl.loop(0, HEADS)
    def _(h):
        for copy in loads(h):
            copy.start()

    for copy in late:
        copy.start()

    barrier = pltpu.get_barrier_semaphore()

    def greet(target):
        pl.semaphore_signal(barrier, inc=1, device_id=(rep, target), device_id_type=MESH)

    greet(partner)

    @pl.when(core == 0)
    def _():
        greet(dev(-2))
        pl.semaphore_wait(barrier, 2)

    @pl.when(core == 1)
    def _():
        greet(dev(-4))

        @pl.when(side == 0)
        def _():
            greet(dev(2))

        @pl.when(side == 1)
        def _():
            greet(dev(-2))

        pl.semaphore_wait(barrier, 3)

    def push(h, source, slot, target, use):
        return pltpu.make_async_remote_copy(
            src_ref=kv.at[source, h],
            dst_ref=kv.at[slot, h],
            send_sem=send_sem.at[use, h],
            recv_sem=recv_sem.at[slot, h],
            device_id=(rep, target),
            device_id_type=MESH,
        )

    def arrived(h, slot):
        push(h, slot, slot, partner, 0).wait_recv()

    def sent(h, use):
        push(h, OWN, OWN, partner, use).wait_send()

    @pl.loop(0, HEADS)
    def _(h):
        for copy in loads(h):
            copy.wait()

        @pl.when(core == 0)
        def _():
            push(h, OWN, TWO_BACK, dev(2), 0).start()
            push(h, OWN, EVEN_OWN, partner, 2).start()

        @pl.when(core == 1)
        def _():
            push(h, OWN, THREE_BACK, dev(4), 1).start()

            @pl.when(side == 0)
            def _():
                push(h, OWN, ONE_BACK, dev(2), 0).start()

    def weigh(q, k):
        half = half_scale * lax.dot_general(
            q, k, (((1,), (1,)), ((), ())), preferred_element_type=jnp.float32
        )
        return half + half * jnp.tanh(half)

    tiles = rows // row_tile
    causal = lax.broadcasted_iota(jnp.int32, (row_tile, row_tile), 1) <= (
        lax.broadcasted_iota(jnp.int32, (row_tile, row_tile), 0)
    )

    def head_columns(h):
        return pl.ds(pl.multiple_of(h * size, size), size)

    @pl.loop(0, HEADS)
    def _(h):
        for tile in range(tiles):
            low, high = tile * row_tile, (tile + 1) * row_tile
            q = queries[h, low:high]
            edge = jnp.where(causal, weigh(q, kv[OWN, h, 0, low:high]), 0.0).astype(jnp.bfloat16)
            total = jnp.dot(edge, kv[OWN, h, 1, low:high], preferred_element_type=jnp.float32)
            if tile:
                full = weigh(q, kv[OWN, h, 0, :low]).astype(jnp.bfloat16)
                total += jnp.dot(full, kv[OWN, h, 1, :low], preferred_element_type=jnp.float32)
            attn[low:high, head_columns(h)] = total

    @pl.loop(0, HEADS + 2)
    def _(step):
        @pl.when(step < HEADS)
        def _():
            h = step

            @pl.when(core == 0)
            def _():
                arrived(h, TWO_BACK)
                push(h, TWO_BACK, TWO_BACK, partner, 3).start()

            @pl.when(core == 1)
            def _():
                arrived(h, THREE_BACK)

                @pl.when(side == 1)
                def _():
                    push(h, THREE_BACK, ONE_BACK, dev(-2), 0).start()

                push(h, THREE_BACK, THREE_BACK, partner, 2).start()

                @pl.when(side == 1)
                def _():
                    arrived(h, ONE_BACK)
                    push(h, ONE_BACK, ONE_BACK, partner, 3).start()

        @pl.when((step >= 1) & (step <= HEADS) & (core == 1) & (side == 0))
        def _():
            h = step - 1
            arrived(h, ONE_BACK)
            push(h, ONE_BACK, ONE_BACK, partner, 3).start()

        @pl.when(step >= 2)
        def _():
            h = step - 2

            @pl.when(core == 0)
            def _():
                arrived(h, ONE_BACK)
                arrived(h, THREE_BACK)

            @pl.when(core == 1)
            def _():
                arrived(h, EVEN_OWN)
                arrived(h, TWO_BACK)

            for tile in range(tiles):
                low, high = tile * row_tile, (tile + 1) * row_tile
                q = queries[h, low:high]
                total = attn[low:high, head_columns(h)]
                for back in range(3):
                    slot = lax.rem(back + 3 * core, 4)
                    w = weigh(q, kv[slot, h, 0]).astype(jnp.bfloat16)
                    part = jnp.dot(w, kv[slot, h, 1], preferred_element_type=jnp.float32)
                    total += jnp.where(flags_ref[back] > 0, part, 0.0)
                attn[low:high, head_columns(h)] = total

    for copy in late:
        copy.wait()
    valid = flags_ref[3]
    gain = gain_ref[...]
    for tile in range(tiles):
        low, high = tile * row_tile, (tile + 1) * row_tile
        ids = low + lax.broadcasted_iota(jnp.int32, (row_tile, 1), 0)
        x = jnp.where(ids < valid, attn[low:high], 0.0)
        centered = x - jnp.mean(x, axis=1, keepdims=True)
        var = jnp.mean(centered * centered, axis=1, keepdims=True)
        normed = centered * lax.rsqrt(var + 1e-06) * gain
        gated = (normed * gates[low:high].astype(jnp.float32)).astype(jnp.bfloat16)
        out = jnp.dot(gated, weights[...], preferred_element_type=jnp.float32)
        out_ref[low:high] = (out + residual[low:high].astype(jnp.float32)).astype(jnp.bfloat16)

    @pl.loop(0, HEADS)
    def _(h):
        sent(h, 2)
        sent(h, 3)

        @pl.when((core == 0) | (side == 0) | (side == 1))
        def _():
            sent(h, 0)

        @pl.when(core == 1)
        def _():
            sent(h, 1)


def history_layer(n, flags, gain, projected, history_in, out_proj):
    rows, width = history_in.shape
    size = width // HEADS
    row_tile = next(t for t in (256, 128, 64, 32, 16, rows) if rows % t == 0)
    anywhere = pl.BlockSpec(memory_space=pl.ANY)
    vmem = pl.BlockSpec(memory_space=pltpu.VMEM)
    return pl.pallas_call(
        functools.partial(history_kernel, n, row_tile),
        out_shape=jax.ShapeDtypeStruct((rows, width), jnp.bfloat16),
        in_specs=[pl.BlockSpec(memory_space=pltpu.SMEM), vmem, anywhere, anywhere, anywhere],
        out_specs=vmem,
        scratch_shapes=[
            pltpu.VMEM((5, HEADS, 2, rows, size), jnp.bfloat16),
            pltpu.VMEM((HEADS, rows, size), jnp.bfloat16),
            pltpu.VMEM((rows, width), jnp.bfloat16),
            pltpu.VMEM((rows, width), jnp.bfloat16),
            pltpu.VMEM((width, width), jnp.bfloat16),
            pltpu.VMEM((rows, width), jnp.float32),
            pltpu.SemaphoreType.DMA((HEADS, 3)),
            pltpu.SemaphoreType.DMA((3,)),
            pltpu.SemaphoreType.DMA((4, HEADS)),
            pltpu.SemaphoreType.DMA((5, HEADS)),
        ],
        compiler_params=pltpu.CompilerParams(
            collective_id=0, has_side_effects=True, vmem_limit_bytes=60 * 1024 * 1024
        ),
        name="history_layer",
    )(flags, gain, projected, history_in, out_proj)


def gather_kernel(n, row_ref, rows_ref, own_sem, send_sem, recv_sem):
    rep, me = lax.axis_index("rep"), lax.axis_index("seq")
    own = pltpu.make_async_copy(row_ref, rows_ref.at[me], own_sem)
    own.start()
    barrier = pltpu.get_barrier_semaphore()

    def copy_to(shift):
        return pltpu.make_async_remote_copy(
            src_ref=row_ref,
            dst_ref=rows_ref.at[me],
            send_sem=send_sem.at[shift],
            recv_sem=recv_sem.at[shift],
            device_id=(rep, lax.rem(me + shift, n)),
            device_id_type=MESH,
        )

    @pl.loop(1, n)
    def _(shift):
        pl.semaphore_signal(
            barrier, inc=1, device_id=(rep, lax.rem(me + shift, n)), device_id_type=MESH
        )

    pl.semaphore_wait(barrier, n - 1)

    @pl.loop(1, n)
    def _(shift):
        copy_to(shift).start()

    own.wait()

    @pl.loop(1, n)
    def _(shift):
        copy_to(shift).wait_send()
        copy_to(shift).wait_recv()


def gather_rows(n, row):
    vmem = pl.BlockSpec(memory_space=pltpu.VMEM)
    width = row.shape[1]
    return pl.pallas_call(
        functools.partial(gather_kernel, n),
        out_shape=jax.ShapeDtypeStruct((n, 1, width), row.dtype),
        in_specs=[vmem],
        out_specs=vmem,
        scratch_shapes=[
            pltpu.SemaphoreType.DMA,
            pltpu.SemaphoreType.DMA((n,)),
            pltpu.SemaphoreType.DMA((n,)),
        ],
        compiler_params=pltpu.CompilerParams(collective_id=1, has_side_effects=True),
        name="gather_rows",
    )(row)


def body(
    projected,
    history_in,
    norm_gain,
    out_proj,
    user_spans,
    user_tails,
    cand_emb,
    cand_user,
    cross_down,
    cross_up,
    cross_bias,
    score_weight,
):
    row_count, model_width = history_in.shape
    devices = lax.axis_size("seq")
    my_index = lax.axis_index("seq")
    span_limit = min(4, devices // 2)
    last_dev = jnp.cumsum(user_spans) - 1
    first_dev = last_dev - user_spans + 1
    device_ids = jnp.arange(devices, dtype=jnp.int32)
    owner_of = jnp.sum((first_dev[None, :] <= device_ids[:, None]).astype(jnp.int32), axis=1) - 1
    is_end = device_ids == last_dev[owner_of]
    valid_rows = jnp.where(is_end, user_tails[owner_of], row_count)
    before = my_index - 1 - jnp.arange(3, dtype=jnp.int32)
    same_user = (before >= 0) & (owner_of[jnp.maximum(before, 0)] == owner_of[my_index])
    same_user &= jnp.arange(1, 4) < span_limit
    valid_here = valid_rows[my_index]
    flags = jnp.concatenate([same_user.astype(jnp.int32), valid_here[None].astype(jnp.int32)])
    history_out = history_layer(
        devices, flags, norm_gain[None, :], projected, history_in, out_proj
    )
    last_row = jnp.where(is_end[my_index], valid_here - 1, 0)
    final_row = lax.dynamic_slice_in_dim(history_out, last_row, 1, 0)
    final_row = jnp.where(is_end[my_index], final_row, jnp.zeros_like(final_row))
    user_rows = gather_rows(devices, final_row.astype(jnp.float32))
    user_rows = user_rows.reshape(devices, model_width).astype(jnp.bfloat16)
    user_count = user_spans.shape[0]
    user_match = cand_user[:, None] == jnp.arange(user_count, dtype=jnp.int32)[None, :]
    cand_dev = jnp.sum(jnp.where(user_match, last_dev[None, :], 0), axis=1)
    selector = (cand_dev[:, None] == device_ids[None, :]).astype(jnp.bfloat16)
    user_part = jnp.dot(selector, user_rows, preferred_element_type=jnp.float32).astype(
        jnp.bfloat16
    )
    crossed_in = jnp.concatenate([user_part, cand_emb], axis=1)
    low_rank = jnp.dot(crossed_in, cross_down, preferred_element_type=jnp.float32).astype(
        jnp.bfloat16
    )
    up_part = jnp.dot(low_rank, cross_up, preferred_element_type=jnp.float32)
    input_float = crossed_in.astype(jnp.float32)
    crossed = input_float * (up_part + cross_bias) + input_float
    scores = jnp.sum(crossed * score_weight, axis=1)
    return (history_out, scores)


def solution(mesh):
    in_specs = (
        P(("rep", "seq"), None),
        P(("rep", "seq"), None),
        P(),
        P(),
        P("rep"),
        P("rep"),
        P(("rep", "seq"), None),
        P(("rep", "seq")),
        P(),
        P(),
        P(),
        P(),
    )
    out_specs = (P(("rep", "seq"), None), P(("rep", "seq")))
    return jax.shard_map(body, mesh=mesh, in_specs=in_specs, out_specs=out_specs, check_vma=False)
```

```python
import functools

import jax
import jax.numpy as jnp
from jax import lax
from jax.experimental import pallas as pl
from jax.experimental.pallas import tpu as pltpu
from jax.sharding import PartitionSpec as P

HEADS = 8
MESH = pl.DeviceIdType.MESH
ONE_BACK, TWO_BACK, THREE_BACK, EVEN_OWN, OWN = range(5)


def history_kernel(
    n, row_tile, spans_ref, tails_ref, gain_ref, proj_ref, hist_ref, weight_ref, out_ref, rows_ref,
    kv, queries, gates, residual, weights, attn, final_row,
    local_sem, side_sem, send_sem, recv_sem, row_send_sem, row_recv_sem,
):
    rep, me = lax.axis_index("rep"), lax.axis_index("seq")
    core = lax.rem(me, 2)
    side = lax.rem(me // 2, 2)
    rows, width = residual.shape
    size = width // HEADS
    half_scale = 0.5 * size ** (-0.5)

    def dev(shift):
        return lax.rem(me + shift + n, n)

    partner = me + 1 - 2 * core

    def load(h, part, target, sem):
        columns = pl.ds(pl.multiple_of(part * width + h * size, size), size)
        return pltpu.make_async_copy(proj_ref.at[:, columns], target, sem)

    def loads(h):
        return (
            load(h, 2, kv.at[OWN, h, 0], local_sem.at[h, 0]),
            load(h, 3, kv.at[OWN, h, 1], local_sem.at[h, 1]),
            load(h, 1, queries.at[h], local_sem.at[h, 2]),
        )

    late = (
        pltpu.make_async_copy(proj_ref.at[:, pl.ds(0, width)], gates, side_sem.at[0]),
        pltpu.make_async_copy(hist_ref, residual, side_sem.at[1]),
        pltpu.make_async_copy(weight_ref, weights, side_sem.at[2]),
    )

    @pl.loop(0, HEADS)
    def _(h):
        for copy in loads(h):
            copy.start()

    for copy in late:
        copy.start()

    barrier = pltpu.get_barrier_semaphore()

    @pl.loop(1, n)
    def _(shift):
        pl.semaphore_signal(
            barrier, inc=1, device_id=(rep, dev(shift)), device_id_type=MESH
        )

    def scan_user(user, found):
        start, first, last, tail = found
        end = start + spans_ref[user]
        mine = (start <= me) & (me < end)
        return (
            end,
            jnp.where(mine, start, first),
            jnp.where(mine, end - 1, last),
            jnp.where(mine, tails_ref[user], tail),
        )

    zero = jnp.int32(0)
    _, first, last, tail = lax.fori_loop(
        0, spans_ref.shape[0], scan_user, (zero, zero, zero, zero)
    )
    valid = jnp.where(me == last, tail, rows)

    pl.semaphore_wait(barrier, n - 1)

    def push(h, source, slot, target, use):
        return pltpu.make_async_remote_copy(
            src_ref=kv.at[source, h],
            dst_ref=kv.at[slot, h],
            send_sem=send_sem.at[use, h],
            recv_sem=recv_sem.at[slot, h],
            device_id=(rep, target),
            device_id_type=MESH,
        )

    def arrived(h, slot):
        push(h, slot, slot, partner, 0).wait_recv()

    def sent(h, use):
        push(h, OWN, OWN, partner, use).wait_send()

    @pl.loop(0, HEADS)
    def _(h):
        for copy in loads(h):
            copy.wait()

        @pl.when(core == 0)
        def _():
            push(h, OWN, TWO_BACK, dev(2), 0).start()
            push(h, OWN, EVEN_OWN, partner, 2).start()

        @pl.when(core == 1)
        def _():
            push(h, OWN, THREE_BACK, dev(4), 1).start()

            @pl.when(side == 0)
            def _():
                push(h, OWN, ONE_BACK, dev(2), 0).start()

    def weigh(q, k):
        half = half_scale * lax.dot_general(
            q, k, (((1,), (1,)), ((), ())), preferred_element_type=jnp.float32
        )
        return half + half * jnp.tanh(half)

    tiles = rows // row_tile
    causal = lax.broadcasted_iota(jnp.int32, (row_tile, row_tile), 1) <= (
        lax.broadcasted_iota(jnp.int32, (row_tile, row_tile), 0)
    )

    def head_columns(h):
        return pl.ds(pl.multiple_of(h * size, size), size)

    @pl.loop(0, HEADS)
    def _(h):
        for tile in range(tiles):
            low, high = tile * row_tile, (tile + 1) * row_tile
            q = queries[h, low:high]
            edge = jnp.where(causal, weigh(q, kv[OWN, h, 0, low:high]), 0.0).astype(jnp.bfloat16)
            total = jnp.dot(edge, kv[OWN, h, 1, low:high], preferred_element_type=jnp.float32)
            if tile:
                full = weigh(q, kv[OWN, h, 0, :low]).astype(jnp.bfloat16)
                total += jnp.dot(full, kv[OWN, h, 1, :low], preferred_element_type=jnp.float32)
            attn[low:high, head_columns(h)] = total

    def absorb(h, blocks):
        for tile in range(tiles):
            low, high = tile * row_tile, (tile + 1) * row_tile
            q = queries[h, low:high]
            total = attn[low:high, head_columns(h)]
            for slot, back in blocks:
                w = weigh(q, kv[slot, h, 0]).astype(jnp.bfloat16)
                part = jnp.dot(w, kv[slot, h, 1], preferred_element_type=jnp.float32)
                total += jnp.where(me - back >= first, part, 0.0)
            attn[low:high, head_columns(h)] = total

    @pl.loop(0, HEADS + 1)
    def _(step):
        @pl.when(step < HEADS)
        def _():
            h = step

            @pl.when(core == 0)
            def _():
                arrived(h, TWO_BACK)
                push(h, TWO_BACK, TWO_BACK, partner, 3).start()

            @pl.when(core == 1)
            def _():
                arrived(h, EVEN_OWN)
                absorb(h, ((EVEN_OWN, 1),))
                arrived(h, THREE_BACK)

                @pl.when(side == 1)
                def _():
                    push(h, THREE_BACK, ONE_BACK, dev(-2), 0).start()

                push(h, THREE_BACK, THREE_BACK, partner, 2).start()

                @pl.when(side == 1)
                def _():
                    arrived(h, ONE_BACK)
                    push(h, ONE_BACK, ONE_BACK, partner, 3).start()

        @pl.when(step >= 1)
        def _():
            h = step - 1

            @pl.when(core == 0)
            def _():
                arrived(h, ONE_BACK)
                arrived(h, THREE_BACK)
                absorb(h, ((ONE_BACK, 1), (TWO_BACK, 2), (THREE_BACK, 3)))

            @pl.when(core == 1)
            def _():
                @pl.when(side == 0)
                def _():
                    arrived(h, ONE_BACK)
                    push(h, ONE_BACK, ONE_BACK, partner, 3).start()

                arrived(h, TWO_BACK)
                absorb(h, ((ONE_BACK, 2), (TWO_BACK, 3)))

    for copy in late:
        copy.wait()
    gain = gain_ref[...]

    def finish(x, gate, rest):
        centered = x - jnp.mean(x, axis=1, keepdims=True)
        var = jnp.mean(centered * centered, axis=1, keepdims=True)
        normed = centered * lax.rsqrt(var + 1e-06) * gain
        gated = (normed * gate.astype(jnp.float32)).astype(jnp.bfloat16)
        out = jnp.dot(gated, weights[...], preferred_element_type=jnp.float32)
        return (out + rest.astype(jnp.float32)).astype(jnp.bfloat16)

    final = jnp.clip(valid - 1, 0, rows - 1)
    at_last = lax.broadcasted_iota(jnp.int32, (16, rows), 1) == final
    pick = jnp.where(at_last, 1.0, 0.0).astype(jnp.bfloat16)
    picked = finish(
        jnp.broadcast_to(attn[pl.ds(final, 1), :], (16, width)),
        jnp.dot(pick, gates[...], preferred_element_type=jnp.float32),
        jnp.dot(pick, residual[...], preferred_element_type=jnp.float32),
    ).astype(jnp.float32)[0:1]
    final_row[...] = picked
    rows_ref[me] = picked

    def row_to(shift):
        return pltpu.make_async_remote_copy(
            src_ref=final_row,
            dst_ref=rows_ref.at[me],
            send_sem=row_send_sem.at[shift],
            recv_sem=row_recv_sem.at[shift],
            device_id=(rep, dev(shift)),
            device_id_type=MESH,
        )

    for tile in range(tiles):
        low, high = tile * row_tile, (tile + 1) * row_tile
        ids = low + lax.broadcasted_iota(jnp.int32, (row_tile, 1), 0)
        x = jnp.where(ids < valid, attn[low:high], 0.0)
        out_ref[low:high] = finish(x, gates[low:high], residual[low:high])
        if tile == 0:

            @pl.loop(1, n)
            def _(shift):
                row_to(shift).start()

    @pl.loop(1, n)
    def _(shift):
        row_to(shift).wait_send()
        row_to(shift).wait_recv()

    @pl.loop(0, HEADS)
    def _(h):
        sent(h, 2)
        sent(h, 3)
        sent(h, 0)

        @pl.when(core == 1)
        def _():
            sent(h, 1)


def history_layer(n, spans, tails, gain, projected, history_in, out_proj):
    rows, width = history_in.shape
    size = width // HEADS
    row_tile = next(t for t in (256, 128, 64, 32, 16, rows) if rows % t == 0)
    smem = pl.BlockSpec(memory_space=pltpu.SMEM)
    anywhere = pl.BlockSpec(memory_space=pl.ANY)
    vmem = pl.BlockSpec(memory_space=pltpu.VMEM)
    return pl.pallas_call(
        functools.partial(history_kernel, n, row_tile),
        out_shape=(
            jax.ShapeDtypeStruct((rows, width), jnp.bfloat16),
            jax.ShapeDtypeStruct((n, 1, width), jnp.float32),
        ),
        in_specs=[smem, smem, vmem, anywhere, anywhere, anywhere],
        out_specs=(vmem, vmem),
        scratch_shapes=[
            pltpu.VMEM((5, HEADS, 2, rows, size), jnp.bfloat16),
            pltpu.VMEM((HEADS, rows, size), jnp.bfloat16),
            pltpu.VMEM((rows, width), jnp.bfloat16),
            pltpu.VMEM((rows, width), jnp.bfloat16),
            pltpu.VMEM((width, width), jnp.bfloat16),
            pltpu.VMEM((rows, width), jnp.float32),
            pltpu.VMEM((1, width), jnp.float32),
            pltpu.SemaphoreType.DMA((HEADS, 3)),
            pltpu.SemaphoreType.DMA((3,)),
            pltpu.SemaphoreType.DMA((4, HEADS)),
            pltpu.SemaphoreType.DMA((5, HEADS)),
            pltpu.SemaphoreType.DMA((n,)),
            pltpu.SemaphoreType.DMA((n,)),
        ],
        compiler_params=pltpu.CompilerParams(
            collective_id=0, has_side_effects=True, vmem_limit_bytes=60 * 1024 * 1024
        ),
        name="history_layer",
    )(spans, tails, gain, projected, history_in, out_proj)


def body(
    projected,
    history_in,
    norm_gain,
    out_proj,
    user_spans,
    user_tails,
    cand_emb,
    cand_user,
    cross_down,
    cross_up,
    cross_bias,
    score_weight,
):
    model_width = history_in.shape[1]
    devices = lax.axis_size("seq")
    history_out, user_rows = history_layer(
        devices, user_spans, user_tails, norm_gain[None, :], projected, history_in, out_proj
    )
    user_rows = user_rows.reshape(devices, model_width).astype(jnp.bfloat16)
    device_ids = jnp.arange(devices, dtype=jnp.int32)
    user_count = user_spans.shape[0]
    users = jnp.arange(user_count, dtype=jnp.int32)
    last_dev = jnp.sum(jnp.where(users[None, :] <= users[:, None], user_spans[None, :], 0), axis=1) - 1
    user_match = cand_user[:, None] == jnp.arange(user_count, dtype=jnp.int32)[None, :]
    cand_dev = jnp.sum(jnp.where(user_match, last_dev[None, :], 0), axis=1)
    selector = (cand_dev[:, None] == device_ids[None, :]).astype(jnp.bfloat16)
    user_part = jnp.dot(selector, user_rows, preferred_element_type=jnp.float32).astype(
        jnp.bfloat16
    )
    crossed_in = jnp.concatenate([user_part, cand_emb], axis=1)
    low_rank = jnp.dot(crossed_in, cross_down, preferred_element_type=jnp.float32).astype(
        jnp.bfloat16
    )
    up_part = jnp.dot(low_rank, cross_up, preferred_element_type=jnp.float32)
    input_float = crossed_in.astype(jnp.float32)
    crossed = input_float * (up_part + cross_bias) + input_float
    scores = jnp.sum(crossed * score_weight, axis=1)
    return (history_out, scores)


def solution(mesh):
    in_specs = (
        P(("rep", "seq"), None),
        P(("rep", "seq"), None),
        P(),
        P(),
        P("rep"),
        P("rep"),
        P(("rep", "seq"), None),
        P(("rep", "seq")),
        P(),
        P(),
        P(),
        P(),
    )
    out_specs = (P(("rep", "seq"), None), P(("rep", "seq")))
    return jax.shard_map(body, mesh=mesh, in_specs=in_specs, out_specs=out_specs, check_vma=False)
```

```python
import functools

import jax
import jax.numpy as jnp
from jax import lax
from jax.experimental import pallas as pl
from jax.experimental.pallas import tpu as pltpu
from jax.sharding import PartitionSpec as P

HEADS = 8
MESH = pl.DeviceIdType.MESH
ONE_BACK, TWO_BACK, THREE_BACK, EVEN_OWN, OWN = range(5)


def history_kernel(
    n, row_tile, spans_ref, tails_ref, gain_ref, proj_ref, hist_ref, weight_ref, out_ref, table_ref,
    kv, queries, gates, residual, weights, attn, final_row, rows_ref,
    local_sem, side_sem, send_sem, recv_sem, row_send_sem, row_recv_sem,
):
    rep, me = lax.axis_index("rep"), lax.axis_index("seq")
    core = lax.rem(me, 2)
    side = lax.rem(me // 2, 2)
    rows, width = residual.shape
    size = width // HEADS
    half_scale = 0.5 * size ** (-0.5)

    def dev(shift):
        return lax.rem(me + shift + n, n)

    partner = me + 1 - 2 * core

    def load(h, part, target, sem):
        columns = pl.ds(pl.multiple_of(part * width + h * size, size), size)
        return pltpu.make_async_copy(proj_ref.at[:, columns], target, sem)

    def loads(h):
        return (
            load(h, 2, kv.at[OWN, h, 0], local_sem.at[h, 0]),
            load(h, 3, kv.at[OWN, h, 1], local_sem.at[h, 1]),
            load(h, 1, queries.at[h], local_sem.at[h, 2]),
        )

    late = (
        pltpu.make_async_copy(proj_ref.at[:, pl.ds(0, width)], gates, side_sem.at[0]),
        pltpu.make_async_copy(hist_ref, residual, side_sem.at[1]),
        pltpu.make_async_copy(weight_ref, weights, side_sem.at[2]),
    )

    @pl.loop(0, HEADS)
    def _(h):
        for copy in loads(h):
            copy.start()

    for copy in late:
        copy.start()

    barrier = pltpu.get_barrier_semaphore()

    @pl.loop(1, n)
    def _(shift):
        pl.semaphore_signal(
            barrier, inc=1, device_id=(rep, dev(shift)), device_id_type=MESH
        )

    def scan_user(user, found):
        start, first, last, tail = found
        end = start + spans_ref[user]
        mine = (start <= me) & (me < end)
        return (
            end,
            jnp.where(mine, start, first),
            jnp.where(mine, end - 1, last),
            jnp.where(mine, tails_ref[user], tail),
        )

    zero = jnp.int32(0)
    _, first, last, tail = lax.fori_loop(
        0, spans_ref.shape[0], scan_user, (zero, zero, zero, zero)
    )
    valid = jnp.where(me == last, tail, rows)

    pl.semaphore_wait(barrier, n - 1)

    def push(h, source, slot, target, use):
        return pltpu.make_async_remote_copy(
            src_ref=kv.at[source, h],
            dst_ref=kv.at[slot, h],
            send_sem=send_sem.at[use, h],
            recv_sem=recv_sem.at[slot, h],
            device_id=(rep, target),
            device_id_type=MESH,
        )

    def arrived(h, slot):
        push(h, slot, slot, partner, 0).wait_recv()

    def sent(h, use):
        push(h, OWN, OWN, partner, use).wait_send()

    @pl.loop(0, HEADS)
    def _(h):
        for copy in loads(h):
            copy.wait()

        @pl.when(core == 0)
        def _():
            push(h, OWN, TWO_BACK, dev(2), 0).start()
            push(h, OWN, EVEN_OWN, partner, 2).start()

        @pl.when(core == 1)
        def _():
            push(h, OWN, THREE_BACK, dev(4), 1).start()

            @pl.when(side == 0)
            def _():
                push(h, OWN, ONE_BACK, dev(2), 0).start()

    def weigh(q, k):
        half = half_scale * lax.dot_general(
            q, k, (((1,), (1,)), ((), ())), preferred_element_type=jnp.float32
        )
        return half + half * jnp.tanh(half)

    tiles = rows // row_tile
    causal = lax.broadcasted_iota(jnp.int32, (row_tile, row_tile), 1) <= (
        lax.broadcasted_iota(jnp.int32, (row_tile, row_tile), 0)
    )

    def head_columns(h):
        return pl.ds(pl.multiple_of(h * size, size), size)

    @pl.loop(0, HEADS)
    def _(h):
        for tile in range(tiles):
            low, high = tile * row_tile, (tile + 1) * row_tile
            q = queries[h, low:high]
            edge = jnp.where(causal, weigh(q, kv[OWN, h, 0, low:high]), 0.0).astype(jnp.bfloat16)
            total = jnp.dot(edge, kv[OWN, h, 1, low:high], preferred_element_type=jnp.float32)
            if tile:
                full = weigh(q, kv[OWN, h, 0, :low]).astype(jnp.bfloat16)
                total += jnp.dot(full, kv[OWN, h, 1, :low], preferred_element_type=jnp.float32)
            attn[low:high, head_columns(h)] = total

    def absorb(h, blocks):
        for tile in range(tiles):
            low, high = tile * row_tile, (tile + 1) * row_tile
            q = queries[h, low:high]
            total = attn[low:high, head_columns(h)]
            for slot, back in blocks:
                w = weigh(q, kv[slot, h, 0]).astype(jnp.bfloat16)
                part = jnp.dot(w, kv[slot, h, 1], preferred_element_type=jnp.float32)
                total += jnp.where(me - back >= first, part, 0.0)
            attn[low:high, head_columns(h)] = total

    @pl.loop(0, HEADS + 1)
    def _(step):
        @pl.when(step < HEADS)
        def _():
            h = step

            @pl.when(core == 0)
            def _():
                arrived(h, TWO_BACK)
                push(h, TWO_BACK, TWO_BACK, partner, 3).start()

            @pl.when(core == 1)
            def _():
                arrived(h, EVEN_OWN)
                absorb(h, ((EVEN_OWN, 1),))
                arrived(h, THREE_BACK)

                @pl.when(side == 1)
                def _():
                    push(h, THREE_BACK, ONE_BACK, dev(-2), 0).start()

                push(h, THREE_BACK, THREE_BACK, partner, 2).start()

                @pl.when(side == 1)
                def _():
                    arrived(h, ONE_BACK)
                    push(h, ONE_BACK, ONE_BACK, partner, 3).start()

        @pl.when(step >= 1)
        def _():
            h = step - 1

            @pl.when(core == 0)
            def _():
                arrived(h, ONE_BACK)
                arrived(h, THREE_BACK)
                absorb(h, ((ONE_BACK, 1), (TWO_BACK, 2), (THREE_BACK, 3)))

            @pl.when(core == 1)
            def _():
                @pl.when(side == 0)
                def _():
                    arrived(h, ONE_BACK)
                    push(h, ONE_BACK, ONE_BACK, partner, 3).start()

                arrived(h, TWO_BACK)
                absorb(h, ((ONE_BACK, 2), (TWO_BACK, 3)))

    for copy in late:
        copy.wait()
    gain = gain_ref[...]

    def finish(x, gate, rest):
        centered = x - jnp.mean(x, axis=1, keepdims=True)
        var = jnp.mean(centered * centered, axis=1, keepdims=True)
        normed = centered * lax.rsqrt(var + 1e-06) * gain
        gated = (normed * gate.astype(jnp.float32)).astype(jnp.bfloat16)
        out = jnp.dot(gated, weights[...], preferred_element_type=jnp.float32)
        return (out + rest.astype(jnp.float32)).astype(jnp.bfloat16)

    final = jnp.clip(valid - 1, 0, rows - 1)
    at_last = lax.broadcasted_iota(jnp.int32, (16, rows), 1) == final
    pick = jnp.where(at_last, 1.0, 0.0).astype(jnp.bfloat16)
    picked = finish(
        jnp.broadcast_to(attn[pl.ds(final, 1), :], (16, width)),
        jnp.dot(pick, gates[...], preferred_element_type=jnp.float32),
        jnp.dot(pick, residual[...], preferred_element_type=jnp.float32),
    ).astype(jnp.float32)[0:1]
    final_row[...] = picked
    rows_ref[me] = picked

    def row_to(shift):
        return pltpu.make_async_remote_copy(
            src_ref=final_row,
            dst_ref=rows_ref.at[me],
            send_sem=row_send_sem.at[shift],
            recv_sem=row_recv_sem.at[shift],
            device_id=(rep, dev(shift)),
            device_id_type=MESH,
        )

    for tile in range(tiles):
        low, high = tile * row_tile, (tile + 1) * row_tile
        ids = low + lax.broadcasted_iota(jnp.int32, (row_tile, 1), 0)
        x = jnp.where(ids < valid, attn[low:high], 0.0)
        out_ref[low:high] = finish(x, gates[low:high], residual[low:high])
        if tile == 0:

            @pl.loop(1, n)
            def _(shift):
                row_to(shift).start()

    @pl.loop(1, n)
    def _(shift):
        row_to(shift).wait_send()
        row_to(shift).wait_recv()

    @pl.loop(0, n)
    def _(index):
        table_ref[pl.ds(index, 1), :] = rows_ref[index]

    @pl.loop(0, HEADS)
    def _(h):
        sent(h, 2)
        sent(h, 3)
        sent(h, 0)

        @pl.when(core == 1)
        def _():
            sent(h, 1)


def history_layer(n, spans, tails, gain, projected, history_in, out_proj):
    rows, width = history_in.shape
    size = width // HEADS
    row_tile = next(t for t in (256, 128, 64, 32, 16, rows) if rows % t == 0)
    smem = pl.BlockSpec(memory_space=pltpu.SMEM)
    anywhere = pl.BlockSpec(memory_space=pl.ANY)
    vmem = pl.BlockSpec(memory_space=pltpu.VMEM)
    return pl.pallas_call(
        functools.partial(history_kernel, n, row_tile),
        out_shape=(
            jax.ShapeDtypeStruct((rows, width), jnp.bfloat16),
            jax.ShapeDtypeStruct((n, width), jnp.float32),
        ),
        in_specs=[smem, smem, vmem, anywhere, anywhere, anywhere],
        out_specs=(vmem, vmem),
        scratch_shapes=[
            pltpu.VMEM((5, HEADS, 2, rows, size), jnp.bfloat16),
            pltpu.VMEM((HEADS, rows, size), jnp.bfloat16),
            pltpu.VMEM((rows, width), jnp.bfloat16),
            pltpu.VMEM((rows, width), jnp.bfloat16),
            pltpu.VMEM((width, width), jnp.bfloat16),
            pltpu.VMEM((rows, width), jnp.float32),
            pltpu.VMEM((1, width), jnp.float32),
            pltpu.VMEM((n, 1, width), jnp.float32),
            pltpu.SemaphoreType.DMA((HEADS, 3)),
            pltpu.SemaphoreType.DMA((3,)),
            pltpu.SemaphoreType.DMA((4, HEADS)),
            pltpu.SemaphoreType.DMA((5, HEADS)),
            pltpu.SemaphoreType.DMA((n,)),
            pltpu.SemaphoreType.DMA((n,)),
        ],
        compiler_params=pltpu.CompilerParams(
            collective_id=0, has_side_effects=True, vmem_limit_bytes=60 * 1024 * 1024
        ),
        name="history_layer",
    )(spans, tails, gain, projected, history_in, out_proj)


def body(
    projected,
    history_in,
    norm_gain,
    out_proj,
    user_spans,
    user_tails,
    cand_emb,
    cand_user,
    cross_down,
    cross_up,
    cross_bias,
    score_weight,
):
    devices = lax.axis_size("seq")
    history_out, user_rows = history_layer(
        devices, user_spans, user_tails, norm_gain[None, :], projected, history_in, out_proj
    )
    user_rows = user_rows.astype(jnp.bfloat16)
    device_ids = jnp.arange(devices, dtype=jnp.int32)
    user_count = user_spans.shape[0]
    users = jnp.arange(user_count, dtype=jnp.int32)
    last_dev = jnp.sum(jnp.where(users[None, :] <= users[:, None], user_spans[None, :], 0), axis=1) - 1
    user_match = cand_user[:, None] == jnp.arange(user_count, dtype=jnp.int32)[None, :]
    cand_dev = jnp.sum(jnp.where(user_match, last_dev[None, :], 0), axis=1)
    selector = (cand_dev[:, None] == device_ids[None, :]).astype(jnp.bfloat16)
    user_part = jnp.dot(selector, user_rows, preferred_element_type=jnp.float32).astype(
        jnp.bfloat16
    )
    crossed_in = jnp.concatenate([user_part, cand_emb], axis=1)
    low_rank = jnp.dot(crossed_in, cross_down, preferred_element_type=jnp.float32).astype(
        jnp.bfloat16
    )
    up_part = jnp.dot(low_rank, cross_up, preferred_element_type=jnp.float32)
    input_float = crossed_in.astype(jnp.float32)
    crossed = input_float * (up_part + cross_bias) + input_float
    scores = jnp.sum(crossed * score_weight, axis=1)
    return (history_out, scores)


def solution(mesh):
    in_specs = (
        P(("rep", "seq"), None),
        P(("rep", "seq"), None),
        P(),
        P(),
        P("rep"),
        P("rep"),
        P(("rep", "seq"), None),
        P(("rep", "seq")),
        P(),
        P(),
        P(),
        P(),
    )
    out_specs = (P(("rep", "seq"), None), P(("rep", "seq")))
    return jax.shard_map(body, mesh=mesh, in_specs=in_specs, out_specs=out_specs, check_vma=False)
```

```python
import functools

import jax
import jax.numpy as jnp
from jax import lax
from jax.experimental import pallas as pl
from jax.experimental.pallas import tpu as pltpu
from jax.sharding import PartitionSpec as P

HEADS = 8
MESH = pl.DeviceIdType.MESH
ONE_BACK, TWO_BACK, THREE_BACK, EVEN_OWN, OWN = range(5)


def history_kernel(
    n, row_tile, spans_ref, tails_ref, gain_ref, proj_ref, hist_ref, weight_ref, out_ref, rows_ref,
    kv, queries, gates, residual, weights, attn, final_row,
    local_sem, side_sem, send_sem, recv_sem, row_send_sem, row_recv_sem,
):
    rep, me = lax.axis_index("rep"), lax.axis_index("seq")
    core = lax.rem(me, 2)
    side = lax.rem(me // 2, 2)
    rows, width = residual.shape
    size = width // HEADS
    half_scale = 0.5 * size ** (-0.5)

    def dev(shift):
        return lax.rem(me + shift + n, n)

    partner = me + 1 - 2 * core

    def load(h, part, target, sem):
        columns = pl.ds(pl.multiple_of(part * width + h * size, size), size)
        return pltpu.make_async_copy(proj_ref.at[:, columns], target, sem)

    def loads(h):
        return (
            load(h, 2, kv.at[OWN, h, 0], local_sem.at[h, 0]),
            load(h, 3, kv.at[OWN, h, 1], local_sem.at[h, 1]),
            load(h, 1, queries.at[h], local_sem.at[h, 2]),
        )

    late = (
        pltpu.make_async_copy(proj_ref.at[:, pl.ds(0, width)], gates, side_sem.at[0]),
        pltpu.make_async_copy(hist_ref, residual, side_sem.at[1]),
        pltpu.make_async_copy(weight_ref, weights, side_sem.at[2]),
    )

    @pl.loop(0, HEADS)
    def _(h):
        for copy in loads(h):
            copy.start()

    for copy in late:
        copy.start()

    barrier = pltpu.get_barrier_semaphore()

    @pl.loop(1, n)
    def _(shift):
        pl.semaphore_signal(
            barrier, inc=1, device_id=(rep, dev(shift)), device_id_type=MESH
        )

    def scan_user(user, found):
        start, first, last, tail = found
        end = start + spans_ref[user]
        mine = (start <= me) & (me < end)
        return (
            end,
            jnp.where(mine, start, first),
            jnp.where(mine, end - 1, last),
            jnp.where(mine, tails_ref[user], tail),
        )

    zero = jnp.int32(0)
    _, first, last, tail = lax.fori_loop(
        0, spans_ref.shape[0], scan_user, (zero, zero, zero, zero)
    )
    valid = jnp.where(me == last, tail, rows)

    pl.semaphore_wait(barrier, n - 1)

    def push(h, source, slot, target, use):
        return pltpu.make_async_remote_copy(
            src_ref=kv.at[source, h],
            dst_ref=kv.at[slot, h],
            send_sem=send_sem.at[use, h],
            recv_sem=recv_sem.at[slot, h],
            device_id=(rep, target),
            device_id_type=MESH,
        )

    def arrived(h, slot):
        push(h, slot, slot, partner, 0).wait_recv()

    def sent(h, use):
        push(h, OWN, OWN, partner, use).wait_send()

    @pl.loop(0, HEADS)
    def _(h):
        for copy in loads(h):
            copy.wait()

        @pl.when(core == 0)
        def _():
            push(h, OWN, TWO_BACK, dev(2), 0).start()
            push(h, OWN, EVEN_OWN, partner, 2).start()

        @pl.when(core == 1)
        def _():
            push(h, OWN, THREE_BACK, dev(4), 1).start()

            @pl.when(side == 0)
            def _():
                push(h, OWN, ONE_BACK, dev(2), 0).start()

    def weigh(q, k):
        half = half_scale * lax.dot_general(
            q, k, (((1,), (1,)), ((), ())), preferred_element_type=jnp.float32
        )
        return half + half * jnp.tanh(half)

    tiles = rows // row_tile
    causal = lax.broadcasted_iota(jnp.int32, (row_tile, row_tile), 1) <= (
        lax.broadcasted_iota(jnp.int32, (row_tile, row_tile), 0)
    )

    def head_columns(h):
        return pl.ds(pl.multiple_of(h * size, size), size)

    @pl.loop(0, HEADS)
    def _(h):
        for tile in range(tiles):
            low, high = tile * row_tile, (tile + 1) * row_tile
            q = queries[h, low:high]
            edge = jnp.where(causal, weigh(q, kv[OWN, h, 0, low:high]), 0.0).astype(jnp.bfloat16)
            total = jnp.dot(edge, kv[OWN, h, 1, low:high], preferred_element_type=jnp.float32)
            if tile:
                full = weigh(q, kv[OWN, h, 0, :low]).astype(jnp.bfloat16)
                total += jnp.dot(full, kv[OWN, h, 1, :low], preferred_element_type=jnp.float32)
            attn[low:high, head_columns(h)] = total

    def absorb(h, blocks):
        for tile in range(tiles):
            low, high = tile * row_tile, (tile + 1) * row_tile
            q = queries[h, low:high]
            total = attn[low:high, head_columns(h)]
            for slot, back in blocks:
                w = weigh(q, kv[slot, h, 0]).astype(jnp.bfloat16)
                part = jnp.dot(w, kv[slot, h, 1], preferred_element_type=jnp.float32)
                total += jnp.where(me - back >= first, part, 0.0)
            attn[low:high, head_columns(h)] = total

    @pl.loop(0, HEADS + 1)
    def _(step):
        @pl.when(step < HEADS)
        def _():
            h = step

            @pl.when(core == 0)
            def _():
                arrived(h, TWO_BACK)
                push(h, TWO_BACK, TWO_BACK, partner, 3).start()

            @pl.when(core == 1)
            def _():
                arrived(h, EVEN_OWN)
                absorb(h, ((EVEN_OWN, 1),))
                arrived(h, THREE_BACK)

                @pl.when(side == 1)
                def _():
                    push(h, THREE_BACK, ONE_BACK, dev(-2), 0).start()

                push(h, THREE_BACK, THREE_BACK, partner, 2).start()

                @pl.when(side == 1)
                def _():
                    arrived(h, ONE_BACK)
                    push(h, ONE_BACK, ONE_BACK, partner, 3).start()

        @pl.when(step >= 1)
        def _():
            h = step - 1

            @pl.when(core == 0)
            def _():
                arrived(h, ONE_BACK)
                arrived(h, THREE_BACK)
                absorb(h, ((ONE_BACK, 1), (TWO_BACK, 2), (THREE_BACK, 3)))

            @pl.when(core == 1)
            def _():
                @pl.when(side == 0)
                def _():
                    arrived(h, ONE_BACK)
                    push(h, ONE_BACK, ONE_BACK, partner, 3).start()

                arrived(h, TWO_BACK)
                absorb(h, ((ONE_BACK, 2), (TWO_BACK, 3)))

    for copy in late:
        copy.wait()
    gain = gain_ref[...]

    def finish(x, gate, rest):
        centered = x - jnp.mean(x, axis=1, keepdims=True)
        var = jnp.mean(centered * centered, axis=1, keepdims=True)
        normed = centered * lax.rsqrt(var + 1e-06) * gain
        gated = (normed * gate.astype(jnp.float32)).astype(jnp.bfloat16)
        out = jnp.dot(gated, weights[...], preferred_element_type=jnp.float32)
        return (out + rest.astype(jnp.float32)).astype(jnp.bfloat16)

    final = jnp.clip(valid - 1, 0, rows - 1)
    at_last = lax.broadcasted_iota(jnp.int32, (16, rows), 1) == final
    pick = jnp.where(at_last, 1.0, 0.0).astype(jnp.bfloat16)
    picked = finish(
        jnp.broadcast_to(attn[pl.ds(final, 1), :], (16, width)),
        jnp.dot(pick, gates[...], preferred_element_type=jnp.float32),
        jnp.dot(pick, residual[...], preferred_element_type=jnp.float32),
    ).astype(jnp.float32)[0:1]
    final_row[...] = picked
    rows_ref[me] = picked

    def row_to(shift):
        return pltpu.make_async_remote_copy(
            src_ref=final_row,
            dst_ref=rows_ref.at[me],
            send_sem=row_send_sem.at[shift],
            recv_sem=row_recv_sem.at[shift],
            device_id=(rep, dev(shift)),
            device_id_type=MESH,
        )

    for tile in range(tiles):
        low, high = tile * row_tile, (tile + 1) * row_tile
        ids = low + lax.broadcasted_iota(jnp.int32, (row_tile, 1), 0)
        x = jnp.where(ids < valid, attn[low:high], 0.0)
        out_ref[low:high] = finish(x, gates[low:high], residual[low:high])
        if tile == 0:

            @pl.loop(1, n)
            def _(shift):
                row_to(shift).start()

    @pl.loop(1, n)
    def _(shift):
        row_to(shift).wait_send()
        row_to(shift).wait_recv()

    @pl.loop(0, HEADS)
    def _(h):
        sent(h, 2)
        sent(h, 3)
        sent(h, 0)

        @pl.when(core == 1)
        def _():
            sent(h, 1)


def history_layer(n, spans, tails, gain, projected, history_in, out_proj):
    rows, width = history_in.shape
    size = width // HEADS
    row_tile = next(t for t in (384, 256, 128, 64, 32, 16, rows) if rows % t == 0)
    smem = pl.BlockSpec(memory_space=pltpu.SMEM)
    anywhere = pl.BlockSpec(memory_space=pl.ANY)
    vmem = pl.BlockSpec(memory_space=pltpu.VMEM)
    return pl.pallas_call(
        functools.partial(history_kernel, n, row_tile),
        out_shape=(
            jax.ShapeDtypeStruct((rows, width), jnp.bfloat16),
            jax.ShapeDtypeStruct((n, 1, width), jnp.float32),
        ),
        in_specs=[smem, smem, vmem, anywhere, anywhere, anywhere],
        out_specs=(vmem, vmem),
        scratch_shapes=[
            pltpu.VMEM((5, HEADS, 2, rows, size), jnp.bfloat16),
            pltpu.VMEM((HEADS, rows, size), jnp.bfloat16),
            pltpu.VMEM((rows, width), jnp.bfloat16),
            pltpu.VMEM((rows, width), jnp.bfloat16),
            pltpu.VMEM((width, width), jnp.bfloat16),
            pltpu.VMEM((rows, width), jnp.float32),
            pltpu.VMEM((1, width), jnp.float32),
            pltpu.SemaphoreType.DMA((HEADS, 3)),
            pltpu.SemaphoreType.DMA((3,)),
            pltpu.SemaphoreType.DMA((4, HEADS)),
            pltpu.SemaphoreType.DMA((5, HEADS)),
            pltpu.SemaphoreType.DMA((n,)),
            pltpu.SemaphoreType.DMA((n,)),
        ],
        compiler_params=pltpu.CompilerParams(
            collective_id=0, has_side_effects=True, vmem_limit_bytes=60 * 1024 * 1024
        ),
        name="history_layer",
    )(spans, tails, gain, projected, history_in, out_proj)


def body(
    projected,
    history_in,
    norm_gain,
    out_proj,
    user_spans,
    user_tails,
    cand_emb,
    cand_user,
    cross_down,
    cross_up,
    cross_bias,
    score_weight,
):
    model_width = history_in.shape[1]
    devices = lax.axis_size("seq")
    history_out, user_rows = history_layer(
        devices, user_spans, user_tails, norm_gain[None, :], projected, history_in, out_proj
    )
    user_rows = user_rows.reshape(devices, model_width).astype(jnp.bfloat16)
    device_ids = jnp.arange(devices, dtype=jnp.int32)
    user_count = user_spans.shape[0]
    users = jnp.arange(user_count, dtype=jnp.int32)
    last_dev = jnp.sum(jnp.where(users[None, :] <= users[:, None], user_spans[None, :], 0), axis=1) - 1
    user_match = cand_user[:, None] == jnp.arange(user_count, dtype=jnp.int32)[None, :]
    cand_dev = jnp.sum(jnp.where(user_match, last_dev[None, :], 0), axis=1)
    selector = (cand_dev[:, None] == device_ids[None, :]).astype(jnp.bfloat16)
    user_part = jnp.dot(selector, user_rows, preferred_element_type=jnp.float32).astype(
        jnp.bfloat16
    )
    crossed_in = jnp.concatenate([user_part, cand_emb], axis=1)
    low_rank = jnp.dot(crossed_in, cross_down, preferred_element_type=jnp.float32).astype(
        jnp.bfloat16
    )
    up_part = jnp.dot(low_rank, cross_up, preferred_element_type=jnp.float32)
    input_float = crossed_in.astype(jnp.float32)
    crossed = input_float * (up_part + cross_bias) + input_float
    scores = jnp.sum(crossed * score_weight, axis=1)
    return (history_out, scores)


def solution(mesh):
    in_specs = (
        P(("rep", "seq"), None),
        P(("rep", "seq"), None),
        P(),
        P(),
        P("rep"),
        P("rep"),
        P(("rep", "seq"), None),
        P(("rep", "seq")),
        P(),
        P(),
        P(),
        P(),
    )
    out_specs = (P(("rep", "seq"), None), P(("rep", "seq")))
    return jax.shard_map(body, mesh=mesh, in_specs=in_specs, out_specs=out_specs, check_vma=False)
```
